256 devices in a mesh: section: 32 (over z_hi, x, core), team: 8 (over y, z_lo).
Axes of the slice: x: 4, y: 4, z: 8 (z_hi: 4, z_lo: 2; z = z_hi * 2 + z_lo), core: 2. Of those that a mesh axis runs over, the one named last changes fastest.
Arguments:
- amps: bfloat16 [4096, 16384], P('team', 'section'), may hold values from -6 to 6
- t_mask: int32 [32, 128], P('team', 'section'), may hold values from 0 to 1, as said below
- ints: bfloat16 [16384, 16384], P('team', 'section'), may hold values from -0.0625 to 0.0625
- v_mask: int32 [128, 128], P('team', 'section'), may hold values 0 or 1
Outputs:
- ladder: bfloat16 [4096, 16384], P('team', 'section')
The draws below stay inside these ranges and needn't reach their ends.
Inputs may be any that keep to these rules, and one draw needn't show every extreme that they name: `t_mask`: in every row of tiles, each aligned group of 4 tile columns holds exactly 2 ones; which ones is random.
All inputs are finite; a program needn't handle non-finite values. No bound on the sum of `v_mask` on one device may be relied on, other than what follows from the above.
Results may differ from the reference program's by a relative error of at most 0.001.
Values may be sent and summed in bfloat16 or wider, within the bound.
No kernel may reach another device: no remote copies, remote signals or barrier semaphores. Data moves between devices by JAX's collectives and lax.ppermute only.
A program may use at most 128 MiB of HBM per device.

```python
import jax
import jax.numpy as jnp
from jax import lax

TILE = 128
PANEL_TILES = 4
NZ = 2
OCC_DEV = 512
VP = 16384
OCC = 4096
AB = 16384


def draw_t_mask(key, part):
    row_tiles = OCC // TILE
    groups = VP // (PANEL_TILES * TILE)
    scores = jax.random.randint(key, (row_tiles, groups, PANEL_TILES), 0, 1 << 20)
    scores = scores * PANEL_TILES + jnp.arange(PANEL_TILES, dtype=jnp.int32)
    order = jnp.argsort(scores, axis=2, stable=True)
    ranks = jnp.argsort(order, axis=2, stable=True)
    chosen = (ranks < NZ).astype(jnp.int32)
    return chosen.reshape(row_tiles, groups * PANEL_TILES)


def set_ends(array, key, low, high):
    spot = [jax.random.randint(jax.random.fold_in(key, axis), (), 0, length) for axis, length in enumerate(array.shape)]
    longest = array.shape.index(max(array.shape))
    next_to = spot[:longest] + [(spot[longest] + 1) % array.shape[longest]] + spot[longest + 1:]
    return array.at[tuple(spot)].set(low).at[tuple(next_to)].set(high)


def levels(own_key, shape, shards, low, top_value):
    loudness = 1.0
    for dim, parts in shards:
        steps = jax.random.uniform(jax.random.fold_in(jax.random.fold_in(own_key, 6), dim), (parts,), jnp.float32, low / len(shards), top_value / len(shards))
        loudness = loudness * jnp.repeat(jnp.exp(steps), shape[dim] // parts).reshape((-1,) + (1,) * (len(shape) - 1 - dim))
    return loudness


def bell_draw(key, extent, deviation, reach, split=(), kind=jnp.bfloat16):
    entries = deviation * jax.random.normal(key, extent, jnp.float32)
    if split:
        entries = entries * levels(key, extent, split, -0.22, 0.18)
    return jnp.clip(entries, -reach, reach).astype(kind)


def setup_inputs(seed: int = 0) -> dict:
    splits = jax.random.split(jax.random.key(seed), 5)
    amps = bell_draw(splits[0], (OCC, VP), 1.0, 6.0, ((0, 8), (1, 32)))
    t_mask = draw_t_mask(jax.random.fold_in(splits[4], 71), 0)
    ints = bell_draw(splits[2], (VP, AB), (VP // 2) ** -0.5, 0.0625, ((0, 8), (1, 32)))
    v_mask = set_ends((jax.random.randint(splits[3], (VP // TILE, AB // TILE), 0, 4) < 3).astype(jnp.int32), jax.random.fold_in(splits[3], 1), 0, 1)
    return {"amps": amps, "t_mask": t_mask, "ints": ints, "v_mask": v_mask}


def expand_mask(values, mask):
    rows, cols = values.shape
    tiles = values.reshape(rows // TILE, TILE, cols // TILE, TILE)
    scaled = tiles * mask.astype(values.dtype)[:, None, :, None]
    return scaled.reshape(rows, cols)


def reference(amps, t_mask, ints, v_mask):
    t_eff = expand_mask(amps, t_mask)
    v_eff = expand_mask(ints, v_mask)
    blocks = t_eff.reshape(OCC // OCC_DEV, OCC_DEV, VP)

    def one_block(block):
        return jnp.dot(block, v_eff, preferred_element_type=jnp.float32).astype(jnp.bfloat16)

    result = lax.map(one_block, blocks)
    return result.reshape(OCC, AB)
```

```python
import jax
import jax.numpy as jnp
from jax import lax
from jax.experimental import pallas as pl
from jax.experimental.pallas import tpu as pltpu
from jax.sharding import Mesh
from jax.sharding import PartitionSpec as P

TILE = 128
NZ = 2
PANEL = 4
ROWS = 512
CODE = 16
BLOCK = ROWS + CODE
WIDTH = NZ * TILE
HALF = ROWS // 2
CHUNKS = (256, 128, 128)
ZH_OF = (1, 3, 2)


def near(x, axis):
    return lax.ppermute(x, axis, [(i, i ^ 1) for i in range(4)])


def wrap(x, axis):
    return lax.ppermute(x, axis, [(i, 3 - i) for i in range(4)])


def swap(x, axis):
    return lax.ppermute(x, axis, [(0, 1), (1, 0)])


def turn(x):
    moves = []
    for hi in range(2):
        for lo in range(2):
            for zl in range(2):
                moves.append(((hi * 2 + lo) * 2 + zl, (zl * 2 + lo) * 2 + hi))
    return lax.ppermute(x, ("x", "zl"), moves)


def ring(x, axis):
    cut = x.shape[0] // 2 // 16 * 16
    one = near(x, axis)
    three = wrap(x, axis)
    top = wrap(one[:cut], axis)
    bottom = near(three[cut:], axis)
    return one, three, top, bottom


def pack_kernel(mask_ref, amps_ref, out_ref):
    lane = lax.broadcasted_iota(jnp.int32, (CODE, WIDTH), 1)
    code = jnp.zeros((CODE, WIDTH), jnp.float32)
    for r in range(PANEL):
        m = [mask_ref[r, c] for c in range(PANEL)]
        first = jnp.where(m[0] == 1, 0, jnp.where(m[1] == 1, 1, 2))
        last = jnp.where(m[3] == 1, 3, jnp.where(m[2] == 1, 2, 1))
        rows = pl.ds(r * TILE, TILE)
        a = [amps_ref[rows, pl.ds(c * TILE, TILE)] for c in range(PANEL)]
        out_ref[rows, pl.ds(0, TILE)] = jnp.where(
            first == 0, a[0], jnp.where(first == 1, a[1], a[2])
        )
        out_ref[rows, pl.ds(TILE, TILE)] = jnp.where(
            last == 3, a[3], jnp.where(last == 2, a[2], a[1])
        )
        code = jnp.where(lane == 2 * r, first.astype(jnp.float32), code)
        code = jnp.where(lane == 2 * r + 1, last.astype(jnp.float32), code)
    out_ref[pl.ds(ROWS, CODE), :] = code.astype(jnp.bfloat16)


def pack(amps, t_mask):
    return pl.pallas_call(
        pack_kernel,
        out_shape=jax.ShapeDtypeStruct((BLOCK, WIDTH), jnp.bfloat16),
        in_specs=[
            pl.BlockSpec(memory_space=pltpu.SMEM),
            pl.BlockSpec(memory_space=pltpu.VMEM),
        ],
        out_specs=pl.BlockSpec(memory_space=pltpu.VMEM),
        compiler_params=pltpu.CompilerParams(vmem_limit_bytes=8 << 20),
        name="pack",
    )(t_mask, amps)


def multiply(flip, group, table, near_parts, far_parts, v_parts):
    width = v_parts[0].shape[1]
    n_a, n_v = len(near_parts), len(v_parts)
    sizes = [p.shape[0] for p in near_parts]
    v_sizes = [p.shape[0] for p in v_parts]

    def kernel(group_ref, table_ref, *refs):
        near_refs, far_refs = refs[:n_a], refs[n_a : 2 * n_a]
        v_refs = refs[2 * n_a : 2 * n_a + n_v]
        out_ref, a_buf, v_buf, a_sem, v_sem = refs[2 * n_a + n_v :]
        which = group_ref[0] ^ flip

        def copies(parts):
            start, made = 0, []
            for i, (ref, size) in enumerate(zip(parts, sizes)):
                made.append(
                    pltpu.make_async_copy(ref, a_buf.at[pl.ds(start, size)], a_sem.at[i])
                )
                start += size
            return made

        start, v_copies = 0, []
        for i, (ref, size) in enumerate(zip(v_refs, v_sizes)):
            v_copies.append(
                pltpu.make_async_copy(ref, v_buf.at[pl.ds(start, size)], v_sem.at[i])
            )
            start += size
        for c in v_copies:
            c.start()

        @pl.when(which == 0)
        def _():
            for c in copies(near_refs):
                c.start()

        @pl.when(which == 1)
        def _():
            for c in copies(far_refs):
                c.start()

        for c in v_copies:
            c.wait()
        for c in copies(near_refs):
            c.wait()
        for r in range(PANEL):
            total = jnp.zeros((TILE, width), jnp.float32)
            for n in range(16):
                spot = ((which * 16 + n) * PANEL + r) * NZ
                v = [
                    v_buf[pl.ds(pl.multiple_of(table_ref[spot + s], TILE), TILE), :]
                    for s in range(NZ)
                ]
                total += jnp.dot(
                    a_buf[pl.ds(n * BLOCK + r * TILE, TILE), :],
                    jnp.concatenate(v, axis=0),
                    preferred_element_type=jnp.float32,
                )
            out_ref[pl.ds(r * TILE, TILE), :] = total

    any_spec = pl.BlockSpec(memory_space=pl.ANY)
    smem = pl.BlockSpec(memory_space=pltpu.SMEM)
    depth = sum(v_sizes)
    return pl.pallas_call(
        kernel,
        out_shape=jax.ShapeDtypeStruct((ROWS, width), jnp.float32),
        in_specs=[smem, smem] + [any_spec] * (2 * n_a + n_v),
        out_specs=pl.BlockSpec(memory_space=pltpu.VMEM),
        scratch_shapes=[
            pltpu.VMEM((16 * BLOCK, WIDTH), jnp.bfloat16),
            pltpu.VMEM((depth, width), jnp.bfloat16),
            pltpu.SemaphoreType.DMA((n_a,)),
            pltpu.SemaphoreType.DMA((n_v,)),
        ],
        compiler_params=pltpu.CompilerParams(vmem_limit_bytes=24 << 20),
        cost_estimate=pl.CostEstimate(
            flops=2 * ROWS * 4096 * width * 2,
            bytes_accessed=2 * (16 * BLOCK * WIDTH + depth * width),
            transcendentals=0,
        ),
        name="multiply",
    )(group, table, *near_parts, *far_parts, *v_parts)


def shards(amps, t_mask, ints, v_mask):
    y, zl = lax.axis_index("y"), lax.axis_index("zl")
    zh, x, core = lax.axis_index("zh"), lax.axis_index("x"), lax.axis_index("core")

    v_chunks = []
    start = 0
    for width in CHUNKS:
        tiles = width // TILE
        part = ints[:, start * TILE : start * TILE + width]
        scale = v_mask[:, start : start + tiles].astype(ints.dtype)
        scale = jnp.repeat(scale, TILE, axis=1)
        part = part.reshape(-1, TILE, width) * scale[:, None, :]
        part = part.reshape(-1, width)
        one, three, top, bottom = ring(part, "y")
        v_chunks.append([part, one, top, bottom, three])
        start += tiles

    own = turn(pack(amps, t_mask))
    x_one, x_three, x_top, x_bottom = ring(own, "x")
    rest = jnp.concatenate(ring(own, "zh"), axis=0)
    r_one, r_three, r_top, r_bottom = ring(rest, "x")
    near_parts = [jnp.concatenate([own, x_one]), rest, r_one]
    far_parts = [
        jnp.concatenate([x_three, x_top, x_bottom]),
        r_three,
        jnp.concatenate([r_top, r_bottom]),
    ]
    near_parts = near_parts + [swap(p, "core") for p in near_parts]
    far_parts = far_parts + [swap(p, "core") for p in far_parts]

    codes = []
    for parts in (near_parts, far_parts):
        for p in parts:
            codes.append(p.reshape(-1, BLOCK, WIDTH)[:, ROWS, : PANEL * NZ])
    codes = jnp.concatenate(codes, axis=0).astype(jnp.int32)
    base = []
    for far in range(2):
        for c in range(2):
            turns = [0, 0] + list(ZH_OF) + list(ZH_OF)
            flips = [far, 1 - far] if not far else [1, 0]
            flips = flips + ([0] * 3 + [1] * 3 if not far else [1] * 3 + [0] * 3)
            for b, f in zip(turns, flips):
                base.append((b ^ zh ^ y) * 4 + ((x & 1) ^ f) * 2 + (core ^ c))
    base = jnp.stack(base) * (PANEL * TILE)
    table = (base[:, None] + codes * TILE).reshape(-1)
    send = jnp.where((x >> 1) == zl, 1, 0).astype(jnp.int32).reshape(1)

    done = []
    for chunk in v_chunks:
        away = multiply(0, send, table, near_parts, far_parts, chunk)
        came = swap(away, "zl")
        kept = multiply(1, send, table, near_parts, far_parts, chunk)
        done.append((kept + came).astype(jnp.bfloat16))
    return jnp.concatenate(done, axis=1)


def solution(mesh):
    split = Mesh(mesh.devices.reshape(4, 4, 2, 4, 2), ("zh", "x", "core", "y", "zl"))
    spec = P(("y", "zl"), ("zh", "x", "core"))
    return jax.shard_map(
        shards, mesh=split, in_specs=(spec,) * 4, out_specs=spec, check_vma=False
    )
```
